512 devices in a mesh: dp: 8 (over x, core), ctx: 64 (over z, y).
Axes of the slice: x: 4, y: 8, z: 8, core: 2. Of those that a mesh axis runs over, the one named last changes fastest.
Arguments:
- queries: bfloat16 [65536, 8192], P(('dp', 'ctx')), parts along dimension 0, may hold values from -6 to 6
- keys: bfloat16 [65536, 1024], P(('dp', 'ctx')), parts along dimension 0, may hold values from -6 to 6
- values: bfloat16 [65536, 1024], P(('dp', 'ctx')), parts along dimension 0, may hold values from -6 to 6
- order: int32 [65536], P('dp'), parts along dimension 0, may hold values from 0 to 8191, each once
- doc_lengths: int32 [128], P('dp'), parts along dimension 0, may hold values from 1 to 1024, 8192 in all
Outputs:
- attended: bfloat16 [65536, 8192], P(('dp', 'ctx')), parts along dimension 0
The draws below stay inside these ranges and needn't reach their ends.
There are 8 independent parts, one for each index of `dp`. The reference program is written for one: setup_inputs(seed, part) draws one part's arguments, and reference() takes and returns one part's arrays. A program takes and returns all parts, laid end to end along the dimension named above; each array names one. Nothing has to cross between parts.
Inputs may be any that keep to these rules, and one draw needn't show every extreme that they name: `order`: each position of the packed sequence stands in exactly one slot. `doc_lengths`: the lengths sum to 8192; the largest is exactly 1024.
All inputs are finite; a program needn't handle non-finite values.
Results may differ from the reference program's by a relative error of at most 0.0046.
Values may be sent and summed in bfloat16 or wider, within the bound.
A program may use at most 128 MiB of HBM per device.

```python
import math
import jax
import jax.numpy as jnp
import numpy as np
from jax import lax

HEADS = 64
KV_HEADS = 8
HEAD_DIM = 128
BLOCK = 512
TOKENS = 8192
DOC_MAX = 1024
NDOCS = 16


def draw_queries(key, part):
    own_key = jax.random.fold_in(key, 11)
    drawn = jnp.clip(jax.random.normal(jax.random.fold_in(own_key, 4), (TOKENS, HEADS, HEAD_DIM), jnp.float32), -6.0, 6.0)
    return drawn.reshape(TOKENS, HEADS * HEAD_DIM).astype(jnp.bfloat16)


def draw_keys(key, part):
    own_key = jax.random.fold_in(key, 21)
    drawn = jnp.clip(jax.random.normal(jax.random.fold_in(own_key, 4), (TOKENS, KV_HEADS, HEAD_DIM), jnp.float32), -6.0, 6.0)
    return drawn.reshape(TOKENS, KV_HEADS * HEAD_DIM).astype(jnp.bfloat16)


def block_scale(key, shape, shards, smallest, largest):
    loudness, own = 1.0, jax.random.fold_in(key, 6)
    for position, shards_of in shards:
        heights = jnp.exp(jax.random.uniform(jax.random.fold_in(own, position), (shards_of,), jnp.float32, smallest / len(shards), largest / len(shards)))
        loudness = loudness * jnp.repeat(heights, shape[position] // shards_of).reshape([-1 if axis == position else 1 for axis in range(len(shape))])
    return loudness


def profile(number_of, total, limit, slope):
    weights = [(1 << 20) // math.isqrt(rank ** slope) + 1 for rank in range(2, number_of + 1)]
    rest, holding = total - limit - (number_of - 1), [1] * (number_of - 1)
    while rest > 0:
        movable = [i for i in range(number_of - 1) if holding[i] < limit]
        mass, left = sum([weights[i] for i in movable]), rest
        for i in movable:
            addition = min(limit - holding[i], max(1, left * weights[i] // mass), rest)
            holding[i] = holding[i] + addition
            rest = rest - addition
    return np.array([limit] + holding)


def uneven(stream_key, count, total, reach, slope):
    if count == 2:
        one = jax.random.randint(stream_key, (), max(1, total - reach), min(reach, total - 1) + 1)
        return jnp.stack([one, total - one])
    sizes = jnp.asarray(profile(count, total, reach, slope), jnp.int32)
    pairs = (count - 1) // 2
    source_of, receiver = sizes[1:1 + 2 * pairs:2], sizes[2:2 + 2 * pairs:2]
    slack = jnp.minimum(source_of - 1, reach - receiver)
    passed = jax.random.randint(jax.random.fold_in(stream_key, 1), (pairs,), 0, 1 << 20) % (slack + 1)
    sizes = sizes.at[1:1 + 2 * pairs:2].set(source_of - passed).at[2:2 + 2 * pairs:2].set(receiver + passed)
    return sizes[jax.random.permutation(jax.random.fold_in(stream_key, 2), count)]


def gaussian(stream_key, extent, width, limit, pieces=(), kind=jnp.bfloat16):
    values = width * jax.random.normal(stream_key, extent, jnp.float32)
    if pieces:
        values = values * block_scale(stream_key, extent, pieces, -0.22, 0.18)
    return jnp.clip(values, -limit, limit).astype(kind)


def setup_inputs(seed: int = 0, part: int = 0) -> dict:
    splits = jax.random.split(jax.random.key(seed), 6)
    own_keys = jax.random.split(jax.random.fold_in(splits[5], part), 6)
    return {
        "queries": draw_queries(jax.random.fold_in(jax.random.fold_in(splits[5], part), 71), part),
        "keys": draw_keys(jax.random.fold_in(jax.random.fold_in(splits[5], part), 71), part),
        "values": gaussian(own_keys[2], (TOKENS, KV_HEADS * HEAD_DIM), 1.0, 6.0, ((0, 64),)),
        "order": jax.random.permutation(own_keys[3], TOKENS).astype(jnp.int32),
        "doc_lengths": uneven(own_keys[4], NDOCS, TOKENS, DOC_MAX, 2).astype(jnp.int32),
    }


def document_starts(doc_lengths):
    doc_ends = jnp.cumsum(doc_lengths).astype(jnp.int32)
    positions = jnp.arange(TOKENS, dtype=jnp.int32)
    doc_index = jnp.sum((positions[:, None] >= doc_ends[None, :]).astype(jnp.int32), axis=1)
    doc_firsts = (doc_ends - doc_lengths).astype(jnp.int32)
    matches = doc_index[:, None] == jnp.arange(NDOCS, dtype=jnp.int32)[None, :]
    return jnp.sum(jnp.where(matches, doc_firsts[None, :], 0), axis=1).astype(jnp.int32)


def attend_head(head_query, head_keys, head_values, doc_start):
    score_scale = HEAD_DIM ** -0.5
    window = DOC_MAX + BLOCK
    padding = jnp.zeros((DOC_MAX, HEAD_DIM), head_keys.dtype)
    padded_keys = jnp.concatenate([padding, head_keys], axis=0)
    padded_values = jnp.concatenate([padding, head_values], axis=0)

    def one_block(block_index):
        block_first = (block_index * BLOCK).astype(jnp.int32)
        query_block = lax.dynamic_slice_in_dim(head_query, block_first, BLOCK, 0)
        key_block = lax.dynamic_slice_in_dim(padded_keys, block_first, window, 0)
        value_block = lax.dynamic_slice_in_dim(padded_values, block_first, window, 0)
        query_pos = block_first + jnp.arange(BLOCK, dtype=jnp.int32)
        key_pos = block_first - DOC_MAX + jnp.arange(window, dtype=jnp.int32)
        start_block = lax.dynamic_slice_in_dim(doc_start, block_first, BLOCK, 0)
        visible = (key_pos[None, :] <= query_pos[:, None]) & (key_pos[None, :] >= start_block[:, None])
        scores = jnp.dot(query_block, key_block.T, preferred_element_type=jnp.float32) * score_scale
        scores = jnp.where(visible, scores, -jnp.inf)
        row_max = jnp.max(scores, axis=1, keepdims=True)
        expo = jnp.exp(scores - row_max)
        row_total = jnp.sum(expo, axis=1, keepdims=True)
        weights = (expo / row_total).astype(jnp.bfloat16)
        return jnp.dot(weights, value_block, preferred_element_type=jnp.float32).astype(jnp.bfloat16)

    blocks = lax.map(one_block, jnp.arange(TOKENS // BLOCK, dtype=jnp.int32))
    return blocks.reshape(TOKENS, HEAD_DIM)


def reference(queries, keys, values, order, doc_lengths):
    slot_of = jnp.zeros((TOKENS,), jnp.int32).at[order].set(jnp.arange(TOKENS, dtype=jnp.int32))
    doc_start = document_starts(doc_lengths)
    natural_q = jnp.take(queries.reshape(TOKENS, HEADS, HEAD_DIM), slot_of, axis=0)
    natural_k = jnp.take(keys.reshape(TOKENS, KV_HEADS, HEAD_DIM), slot_of, axis=0)
    natural_v = jnp.take(values.reshape(TOKENS, KV_HEADS, HEAD_DIM), slot_of, axis=0)
    group_size = HEADS // KV_HEADS

    def one_head(head_index):
        kv_index = (head_index // group_size).astype(jnp.int32)
        head_query = lax.dynamic_index_in_dim(natural_q, head_index, 1, keepdims=False)
        head_keys = lax.dynamic_index_in_dim(natural_k, kv_index, 1, keepdims=False)
        head_values = lax.dynamic_index_in_dim(natural_v, kv_index, 1, keepdims=False)
        return attend_head(head_query, head_keys, head_values, doc_start)

    context = lax.map(one_head, jnp.arange(HEADS, dtype=jnp.int32))
    context = jnp.transpose(context, (1, 0, 2))
    attended = jnp.take(context, order, axis=0)
    return attended.reshape(TOKENS, HEADS * HEAD_DIM)
```

```python
import jax
import jax.numpy as jnp
from jax import lax
from jax.sharding import Mesh
from jax.sharding import PartitionSpec as P

HEADS = 64
KV_HEADS = 8
HEAD_DIM = 128
BLOCK = 512


def document_starts(doc_lengths, tokens):
    doc_count = doc_lengths.shape[0]
    doc_ends = jnp.cumsum(doc_lengths)
    positions = jnp.arange(tokens, dtype=jnp.int32)
    doc_index = jnp.sum((positions[:, None] >= doc_ends[None, :]).astype(jnp.int32), axis=1)
    doc_firsts = doc_ends - doc_lengths
    matches = doc_index[:, None] == jnp.arange(doc_count, dtype=jnp.int32)[None, :]
    return jnp.sum(jnp.where(matches, doc_firsts[None, :], 0), axis=1)


def attend_blocks(q_pos, k_pad, v_pad, doc_start, doc_most, tokens):
    score_scale = HEAD_DIM ** (-0.5)
    window = doc_most + BLOCK
    outs = []
    for block_index in range(tokens // BLOCK):
        block_first = block_index * BLOCK
        query_block = q_pos[block_first : block_first + BLOCK]
        key_block = k_pad[block_first : block_first + window]
        value_block = v_pad[block_first : block_first + window]
        query_pos = block_first + jnp.arange(BLOCK, dtype=jnp.int32)
        key_pos = block_first - doc_most + jnp.arange(window, dtype=jnp.int32)
        start_block = doc_start[block_first : block_first + BLOCK]
        visible = (key_pos[None, :] <= query_pos[:, None]) & (
            key_pos[None, :] >= start_block[:, None]
        )
        scores = (
            jnp.dot(query_block, key_block.T, preferred_element_type=jnp.float32) * score_scale
        )
        scores = jnp.where(visible, scores, -jnp.inf)
        row_max = jnp.max(scores, axis=1, keepdims=True)
        expo = jnp.exp(scores - row_max)
        row_total = jnp.sum(expo, axis=1, keepdims=True)
        weights = (expo / row_total).astype(jnp.bfloat16)
        outs.append(
            jnp.dot(weights, value_block, preferred_element_type=jnp.float32).astype(jnp.bfloat16)
        )
    return jnp.concatenate(outs, axis=0)


def per_device(queries, keys, values, order, doc_lengths):
    nz = lax.axis_size("z")
    ny = lax.axis_size("y")
    tok_rows = queries.shape[0]
    tokens = tok_rows * nz * ny
    query_split = queries.reshape(tok_rows, HEADS, HEAD_DIM)
    query_heads = lax.all_to_all(query_split, ("z", "y"), split_axis=1, concat_axis=0, tiled=True)
    q_slots = query_heads.reshape(tokens, HEAD_DIM)
    paired = jnp.stack(
        [keys.reshape(tok_rows, KV_HEADS, HEAD_DIM), values.reshape(tok_rows, KV_HEADS, HEAD_DIM)],
        axis=2,
    )
    kv_col = lax.all_to_all(paired, "z", split_axis=1, concat_axis=0, tiled=True)
    kv_ring = lax.all_gather(kv_col, "y", axis=0, tiled=True).reshape(tokens, 2 * HEAD_DIM)
    doc_most = tokens // 8
    slot_ids = jnp.arange(tokens, dtype=jnp.int32)
    _, slot_of = lax.sort((order, slot_ids), num_keys=1)
    slot_dev = slot_of // tok_rows
    kv_row = (slot_dev % ny) * (nz * tok_rows) + (slot_dev // ny) * tok_rows + slot_of % tok_rows
    q_pos = jnp.take(q_slots, slot_of, axis=0)
    padded_row = jnp.concatenate([jnp.zeros((doc_most,), jnp.int32), kv_row], axis=0)
    kv_pos = jnp.take(kv_ring, padded_row, axis=0)
    k_pad = kv_pos[:, :HEAD_DIM]
    v_pad = kv_pos[:, HEAD_DIM:]
    doc_start = document_starts(doc_lengths, tokens)
    context = attend_blocks(q_pos, k_pad, v_pad, doc_start, doc_most, tokens)
    slotted = jnp.take(context, order, axis=0)
    returned = lax.all_to_all(slotted, ("z", "y"), split_axis=0, concat_axis=1, tiled=True)
    return returned.reshape(tok_rows, HEADS * HEAD_DIM)


def solution(mesh):
    dp_size, ctx_size = mesh.devices.shape
    grid = Mesh(mesh.devices.reshape(dp_size, KV_HEADS, ctx_size // KV_HEADS), ("dp", "z", "y"))
    rows = P(("dp", "z", "y"), None)
    placed = (rows, rows, rows, P("dp"), P("dp"))
    return jax.shard_map(per_device, mesh=grid, in_specs=placed, out_specs=rows, check_vma=False)
```

```python
import jax
import jax.numpy as jnp
from jax import lax
from jax.sharding import Mesh
from jax.sharding import PartitionSpec as P

HEADS = 64
KV_HEADS = 8
HEAD_DIM = 128
BLOCK = 512


def document_starts(doc_lengths, tokens):
    doc_count = doc_lengths.shape[0]
    doc_ends = jnp.cumsum(doc_lengths)
    positions = jnp.arange(tokens, dtype=jnp.int32)
    doc_index = jnp.sum((positions[:, None] >= doc_ends[None, :]).astype(jnp.int32), axis=1)
    doc_firsts = doc_ends - doc_lengths
    matches = doc_index[:, None] == jnp.arange(doc_count, dtype=jnp.int32)[None, :]
    return jnp.sum(jnp.where(matches, doc_firsts[None, :], 0), axis=1)


def attend_blocks(q_pos, k_pos, v_pos, doc_start, doc_most, tokens):
    score_scale = HEAD_DIM ** (-0.5)
    outs = []
    for block_index in range(tokens // BLOCK):
        block_first = block_index * BLOCK
        key_first = max(block_first - doc_most, 0)
        key_last = block_first + BLOCK
        query_block = q_pos[block_first:key_last]
        key_block = k_pos[key_first:key_last]
        value_block = v_pos[key_first:key_last]
        query_pos = block_first + jnp.arange(BLOCK, dtype=jnp.int32)
        key_pos = key_first + jnp.arange(key_last - key_first, dtype=jnp.int32)
        start_block = doc_start[block_first:key_last]
        visible = (key_pos[None, :] <= query_pos[:, None]) & (
            key_pos[None, :] >= start_block[:, None]
        )
        scores = (
            jnp.dot(query_block, key_block.T, preferred_element_type=jnp.float32) * score_scale
        )
        scores = jnp.where(visible, scores, -jnp.inf)
        row_max = jnp.max(scores, axis=1, keepdims=True)
        expo = jnp.exp(scores - row_max)
        row_total = jnp.sum(expo, axis=1, keepdims=True)
        weights = (expo / row_total).astype(jnp.bfloat16)
        outs.append(
            jnp.dot(weights, value_block, preferred_element_type=jnp.float32).astype(jnp.bfloat16)
        )
    return jnp.concatenate(outs, axis=0)


def per_device(queries, keys, values, order, doc_lengths):
    nz = lax.axis_size("z")
    ny = lax.axis_size("y")
    tok_rows = queries.shape[0]
    tokens = tok_rows * nz * ny
    query_split = queries.reshape(tok_rows, HEADS, HEAD_DIM)
    query_heads = lax.all_to_all(query_split, ("z", "y"), split_axis=1, concat_axis=0, tiled=True)
    q_slots = query_heads.reshape(nz, ny, tok_rows, HEAD_DIM)
    q_ring = jnp.transpose(q_slots, (1, 0, 2, 3)).reshape(tokens, HEAD_DIM)
    paired = jnp.stack(
        [keys.reshape(tok_rows, KV_HEADS, HEAD_DIM), values.reshape(tok_rows, KV_HEADS, HEAD_DIM)],
        axis=2,
    )
    kv_col = lax.all_to_all(paired, "z", split_axis=1, concat_axis=0, tiled=True)
    kv_ring = lax.all_gather(kv_col, "y", axis=0, tiled=True).reshape(tokens, 2 * HEAD_DIM)
    joined = jnp.concatenate([q_ring, kv_ring], axis=1)
    doc_most = tokens // 8
    slot_ids = jnp.arange(tokens, dtype=jnp.int32)
    _, slot_of = lax.sort((order, slot_ids), num_keys=1)
    slot_dev = slot_of // tok_rows
    ring_row = (slot_dev % ny) * (nz * tok_rows) + (slot_dev // ny) * tok_rows + slot_of % tok_rows
    pos_rows = joined.at[ring_row].get(mode="promise_in_bounds", unique_indices=True)
    q_pos = pos_rows[:, :HEAD_DIM]
    k_pos = pos_rows[:, HEAD_DIM : 2 * HEAD_DIM]
    v_pos = pos_rows[:, 2 * HEAD_DIM :]
    doc_start = document_starts(doc_lengths, tokens)
    context = attend_blocks(q_pos, k_pos, v_pos, doc_start, doc_most, tokens)
    slotted = context.at[order].get(mode="promise_in_bounds", unique_indices=True)
    returned = lax.all_to_all(slotted, ("z", "y"), split_axis=0, concat_axis=1, tiled=True)
    return returned.reshape(tok_rows, HEADS * HEAD_DIM)


def solution(mesh):
    dp_size, ctx_size = mesh.devices.shape
    grid = Mesh(mesh.devices.reshape(dp_size, KV_HEADS, ctx_size // KV_HEADS), ("dp", "z", "y"))
    rows = P(("dp", "z", "y"), None)
    placed = (rows, rows, rows, P("dp"), P("dp"))
    return jax.shard_map(per_device, mesh=grid, in_specs=placed, out_specs=rows, check_vma=False)
```

```python
import functools

import jax
import jax.numpy as jnp
from jax import lax
from jax.experimental import pallas as pl
from jax.sharding import Mesh
from jax.sharding import PartitionSpec as P

HEADS = 64
KV_HEADS = 8
HEAD_DIM = 128
BLOCK = 512


def document_starts(doc_lengths, tokens):
    doc_count = doc_lengths.shape[0]
    doc_ends = jnp.cumsum(doc_lengths)
    positions = jnp.arange(tokens, dtype=jnp.int32)
    doc_index = jnp.sum((positions[:, None] >= doc_ends[None, :]).astype(jnp.int32), axis=1)
    doc_firsts = doc_ends - doc_lengths
    matches = doc_index[:, None] == jnp.arange(doc_count, dtype=jnp.int32)[None, :]
    return jnp.sum(jnp.where(matches, doc_firsts[None, :], 0), axis=1)


def attn_kernel(doc_most, q_ref, k_ref, v_ref, ds_ref, o_ref):
    b = pl.program_id(0)
    window = doc_most + BLOCK
    start = pl.multiple_of(jnp.maximum(b * BLOCK - doc_most, 0), BLOCK)
    q = q_ref[...]
    k = k_ref[pl.ds(start, window), :]
    v = v_ref[pl.ds(start, window), :]
    s = lax.dot_general(q, k, (((1,), (1,)), ((), ())), preferred_element_type=jnp.float32)
    s = s * (HEAD_DIM ** (-0.5))
    qpos = b * BLOCK + lax.broadcasted_iota(jnp.int32, (BLOCK, window), 0)
    kpos = start + lax.broadcasted_iota(jnp.int32, (BLOCK, window), 1)
    visible = (kpos <= qpos) & (kpos >= ds_ref[...])
    s = jnp.where(visible, s, -jnp.inf)
    m = jnp.max(s, axis=1, keepdims=True)
    e = jnp.exp(s - m)
    l = jnp.sum(e, axis=1, keepdims=True)
    w = (e / l).astype(jnp.bfloat16)
    o_ref[...] = jnp.dot(w, v, preferred_element_type=jnp.float32).astype(o_ref.dtype)

def attend(q, k, v, doc_start, doc_most):
    tokens = q.shape[0]
    return pl.pallas_call(
        functools.partial(attn_kernel, doc_most),
        grid=(tokens // BLOCK,),
        in_specs=[
            pl.BlockSpec((BLOCK, HEAD_DIM), lambda b: (b, 0)),
            pl.BlockSpec((tokens, HEAD_DIM), lambda b: (0, 0)),
            pl.BlockSpec((tokens, HEAD_DIM), lambda b: (0, 0)),
            pl.BlockSpec((BLOCK, 1), lambda b: (b, 0)),
        ],
        out_specs=pl.BlockSpec((BLOCK, HEAD_DIM), lambda b: (b, 0)),
        out_shape=jax.ShapeDtypeStruct((tokens, HEAD_DIM), jnp.bfloat16),
    )(q, k, v, doc_start.reshape(tokens, 1))


def per_device(queries, keys, values, order, doc_lengths):
    nz = lax.axis_size("z")
    ny = lax.axis_size("y")
    tok_rows = queries.shape[0]
    tokens = tok_rows * nz * ny
    query_split = queries.reshape(tok_rows, HEADS, HEAD_DIM)
    query_heads = lax.all_to_all(query_split, ("z", "y"), split_axis=1, concat_axis=0, tiled=True)
    q_slots = query_heads.reshape(nz, ny, tok_rows, HEAD_DIM)
    q_ring = jnp.transpose(q_slots, (1, 0, 2, 3)).reshape(tokens, HEAD_DIM)
    paired = jnp.stack(
        [keys.reshape(tok_rows, KV_HEADS, HEAD_DIM), values.reshape(tok_rows, KV_HEADS, HEAD_DIM)],
        axis=2,
    )
    kv_col = lax.all_to_all(paired, "z", split_axis=1, concat_axis=0, tiled=True)
    kv_ring = lax.all_gather(kv_col, "y", axis=0, tiled=True).reshape(tokens, 2 * HEAD_DIM)
    joined = jnp.concatenate([q_ring, kv_ring], axis=1)
    doc_most = tokens // 8
    slot_ids = jnp.arange(tokens, dtype=jnp.int32)
    _, slot_of = lax.sort((order, slot_ids), num_keys=1)
    slot_dev = slot_of // tok_rows
    ring_row = (slot_dev % ny) * (nz * tok_rows) + (slot_dev // ny) * tok_rows + slot_of % tok_rows
    pos_rows = joined.at[ring_row].get(mode="promise_in_bounds", unique_indices=True)
    q_pos = pos_rows[:, :HEAD_DIM]
    k_pos = pos_rows[:, HEAD_DIM : 2 * HEAD_DIM]
    v_pos = pos_rows[:, 2 * HEAD_DIM :]
    doc_start = document_starts(doc_lengths, tokens)
    context = attend(q_pos, k_pos, v_pos, doc_start, doc_most)
    slotted = context.at[order].get(mode="promise_in_bounds", unique_indices=True)
    returned = lax.all_to_all(slotted, ("z", "y"), split_axis=0, concat_axis=1, tiled=True)
    return returned.reshape(tok_rows, HEADS * HEAD_DIM)


def solution(mesh):
    dp_size, ctx_size = mesh.devices.shape
    grid = Mesh(mesh.devices.reshape(dp_size, KV_HEADS, ctx_size // KV_HEADS), ("dp", "z", "y"))
    rows = P(("dp", "z", "y"), None)
    placed = (rows, rows, rows, P("dp"), P("dp"))
    return jax.shard_map(per_device, mesh=grid, in_specs=placed, out_specs=rows, check_vma=False)
```

```python
import functools

import jax
import jax.numpy as jnp
from jax import lax
from jax.experimental import pallas as pl
from jax.experimental.pallas import tpu as pltpu
from jax.sharding import Mesh
from jax.sharding import PartitionSpec as P

HEADS = 64
KV_HEADS = 8
HEAD_DIM = 128
BLOCK = 512


def document_starts(doc_lengths, tokens):
    doc_count = doc_lengths.shape[0]
    doc_ends = jnp.cumsum(doc_lengths)
    positions = jnp.arange(tokens, dtype=jnp.int32)
    doc_index = jnp.sum((positions[:, None] >= doc_ends[None, :]).astype(jnp.int32), axis=1)
    doc_firsts = doc_ends - doc_lengths
    matches = doc_index[:, None] == jnp.arange(doc_count, dtype=jnp.int32)[None, :]
    return jnp.sum(jnp.where(matches, doc_firsts[None, :], 0), axis=1)


def attn_kernel(doc_most, first_ref, q_ref, k_ref, v_ref, ds_ref, o_ref, s_scr, m_scr, l_scr, acc_scr):
    b = pl.program_id(0)
    tiles = doc_most // BLOCK + 1
    start = pl.multiple_of(jnp.maximum(b * BLOCK - doc_most, 0), BLOCK)
    q_first = b * BLOCK
    ds_first = first_ref[b]
    q = q_ref[...]
    qpos = q_first + lax.broadcasted_iota(jnp.int32, (BLOCK, BLOCK), 0)
    ds = ds_ref[...]
    m_scr[...] = jnp.full(m_scr.shape, -jnp.inf, jnp.float32)
    l_scr[...] = jnp.zeros(l_scr.shape, jnp.float32)
    acc_scr[...] = jnp.zeros(acc_scr.shape, jnp.float32)
    needed = []
    for t in range(tiles):
        key_first = start + t * BLOCK
        needed.append((key_first + BLOCK - 1 >= ds_first) & (key_first <= q_first + BLOCK - 1))
    for t in range(tiles):
        key_first = start + t * BLOCK

        @pl.when(needed[t])
        def _():
            k = k_ref[pl.ds(pl.multiple_of(key_first, BLOCK), BLOCK), :]
            s = lax.dot_general(q, k, (((1,), (1,)), ((), ())), preferred_element_type=jnp.float32)
            s = s * (HEAD_DIM ** (-0.5))
            kpos = key_first + lax.broadcasted_iota(jnp.int32, (BLOCK, BLOCK), 1)
            s = jnp.where((kpos <= qpos) & (kpos >= ds), s, -jnp.inf)
            s_scr[t] = s
            m_scr[...] = jnp.maximum(m_scr[...], jnp.max(s, axis=1, keepdims=True))
    for t in range(tiles):
        @pl.when(needed[t])
        def _():
            e = jnp.exp(s_scr[t] - m_scr[...])
            s_scr[t] = e
            l_scr[...] += jnp.sum(e, axis=1, keepdims=True)
    for t in range(tiles):
        key_first = start + t * BLOCK

        @pl.when(needed[t])
        def _():
            v = v_ref[pl.ds(pl.multiple_of(key_first, BLOCK), BLOCK), :]
            w = (s_scr[t] / l_scr[...]).astype(jnp.bfloat16)
            acc_scr[...] += jnp.dot(w, v, preferred_element_type=jnp.float32)
    o_ref[...] = acc_scr[...].astype(o_ref.dtype)


def attend(rows, doc_start, doc_most):
    tokens = rows.shape[0]
    tiles = doc_most // BLOCK + 1
    grid_spec = pltpu.PrefetchScalarGridSpec(
        num_scalar_prefetch=1,
        grid=(tokens // BLOCK,),
        in_specs=[
            pl.BlockSpec((BLOCK, HEAD_DIM), lambda b, f: (b, 0)),
            pl.BlockSpec((tokens, HEAD_DIM), lambda b, f: (0, 1)),
            pl.BlockSpec((tokens, HEAD_DIM), lambda b, f: (0, 2)),
            pl.BlockSpec((BLOCK, 1), lambda b, f: (b, 0)),
        ],
        out_specs=pl.BlockSpec((BLOCK, HEAD_DIM), lambda b, f: (b, 0)),
        scratch_shapes=[
            pltpu.VMEM((tiles, BLOCK, BLOCK), jnp.float32),
            pltpu.VMEM((BLOCK, 1), jnp.float32),
            pltpu.VMEM((BLOCK, 1), jnp.float32),
            pltpu.VMEM((BLOCK, HEAD_DIM), jnp.float32),
        ],
    )
    block_firsts = doc_start.reshape(tokens // BLOCK, BLOCK)[:, 0]
    return pl.pallas_call(
        functools.partial(attn_kernel, doc_most),
        grid_spec=grid_spec,
        out_shape=jax.ShapeDtypeStruct((tokens, HEAD_DIM), jnp.bfloat16),
    )(block_firsts, rows, rows, rows, doc_start.reshape(tokens, 1))


def per_device(queries, keys, values, order, doc_lengths):
    nz = lax.axis_size("z")
    ny = lax.axis_size("y")
    tok_rows = queries.shape[0]
    tokens = tok_rows * nz * ny
    query_split = queries.reshape(tok_rows, HEADS, HEAD_DIM)
    query_heads = lax.all_to_all(query_split, ("z", "y"), split_axis=1, concat_axis=0, tiled=True)
    q_slots = query_heads.reshape(nz, ny, tok_rows, HEAD_DIM)
    q_ring = jnp.transpose(q_slots, (1, 0, 2, 3)).reshape(tokens, HEAD_DIM)
    paired = jnp.stack(
        [keys.reshape(tok_rows, KV_HEADS, HEAD_DIM), values.reshape(tok_rows, KV_HEADS, HEAD_DIM)],
        axis=2,
    )
    kv_col = lax.all_to_all(paired, "z", split_axis=1, concat_axis=0, tiled=True)
    kv_ring = lax.all_gather(kv_col, "y", axis=0, tiled=True).reshape(tokens, 2 * HEAD_DIM)
    joined = jnp.concatenate([q_ring, kv_ring], axis=1)
    doc_most = tokens // 8
    slot_ids = jnp.arange(tokens, dtype=jnp.int32)
    _, slot_of = lax.sort((order, slot_ids), num_keys=1)
    slot_dev = slot_of // tok_rows
    ring_row = (slot_dev % ny) * (nz * tok_rows) + (slot_dev // ny) * tok_rows + slot_of % tok_rows
    pos_rows = joined.at[ring_row].get(mode="promise_in_bounds", unique_indices=True)
    doc_start = document_starts(doc_lengths, tokens)
    context = attend(pos_rows, doc_start, doc_most)
    slotted = context.at[order].get(mode="promise_in_bounds", unique_indices=True)
    returned = lax.all_to_all(slotted, ("z", "y"), split_axis=0, concat_axis=1, tiled=True)
    return returned.reshape(tok_rows, HEADS * HEAD_DIM)


def solution(mesh):
    dp_size, ctx_size = mesh.devices.shape
    grid = Mesh(mesh.devices.reshape(dp_size, KV_HEADS, ctx_size // KV_HEADS), ("dp", "z", "y"))
    rows = P(("dp", "z", "y"), None)
    placed = (rows, rows, rows, P("dp"), P("dp"))
    return jax.shard_map(per_device, mesh=grid, in_specs=placed, out_specs=rows, check_vma=False)
```

```python
import functools

import jax
import jax.numpy as jnp
from jax import lax
from jax.experimental import pallas as pl
from jax.experimental.pallas import tpu as pltpu
from jax.sharding import Mesh
from jax.sharding import PartitionSpec as P

HEADS = 64
KV_HEADS = 8
HEAD_DIM = 128
BLOCK = 512


def document_starts(doc_lengths, tokens):
    doc_count = doc_lengths.shape[0]
    doc_ends = jnp.cumsum(doc_lengths)
    positions = jnp.arange(tokens, dtype=jnp.int32)
    doc_index = jnp.sum((positions[:, None] >= doc_ends[None, :]).astype(jnp.int32), axis=1)
    doc_firsts = doc_ends - doc_lengths
    matches = doc_index[:, None] == jnp.arange(doc_count, dtype=jnp.int32)[None, :]
    return jnp.sum(jnp.where(matches, doc_firsts[None, :], 0), axis=1)


def attn_kernel(doc_most, first_ref, q_ref, k_ref, v_ref, ds_ref, o_ref, s_scr, m_scr, l_scr, acc_scr):
    b = pl.program_id(0)
    tiles = doc_most // BLOCK + 1
    start = pl.multiple_of(jnp.maximum(b * BLOCK - doc_most, 0), BLOCK)
    q_first = b * BLOCK
    ds_first = first_ref[b]
    q = q_ref[...]
    qpos = q_first + lax.broadcasted_iota(jnp.int32, (BLOCK, BLOCK), 0)
    ds = ds_ref[...]
    m_scr[...] = jnp.full(m_scr.shape, -jnp.inf, jnp.float32)
    l_scr[...] = jnp.zeros(l_scr.shape, jnp.float32)
    acc_scr[...] = jnp.zeros(acc_scr.shape, jnp.float32)
    needed = []
    for t in range(tiles):
        key_first = start + t * BLOCK
        needed.append((key_first + BLOCK - 1 >= ds_first) & (key_first <= q_first + BLOCK - 1))
    for t in range(tiles):
        key_first = start + t * BLOCK

        @pl.when(needed[t])
        def _():
            k = k_ref[pl.ds(pl.multiple_of(key_first, BLOCK), BLOCK), :]
            s = lax.dot_general(q, k, (((1,), (1,)), ((), ())), preferred_element_type=jnp.float32)
            s = s * (HEAD_DIM ** (-0.5))
            kpos = key_first + lax.broadcasted_iota(jnp.int32, (BLOCK, BLOCK), 1)
            s = jnp.where((kpos <= qpos) & (kpos >= ds), s, -jnp.inf)
            s_scr[t] = s
            m_scr[...] = jnp.maximum(m_scr[...], jnp.max(s, axis=1, keepdims=True))
    for t in range(tiles):
        @pl.when(needed[t])
        def _():
            e = jnp.exp(s_scr[t] - m_scr[...])
            s_scr[t] = e
            l_scr[...] += jnp.sum(e, axis=1, keepdims=True)
    l_scr[...] = 1.0 / l_scr[...]
    for t in range(tiles):
        key_first = start + t * BLOCK

        @pl.when(needed[t])
        def _():
            v = v_ref[pl.ds(pl.multiple_of(key_first, BLOCK), BLOCK), :]
            w = (s_scr[t] * l_scr[...]).astype(jnp.bfloat16)
            acc_scr[...] += jnp.dot(w, v, preferred_element_type=jnp.float32)
    o_ref[...] = acc_scr[...].astype(o_ref.dtype)


def attend(rows, doc_start, doc_most):
    tokens = rows.shape[0]
    tiles = doc_most // BLOCK + 1
    grid_spec = pltpu.PrefetchScalarGridSpec(
        num_scalar_prefetch=1,
        grid=(tokens // BLOCK,),
        in_specs=[
            pl.BlockSpec((BLOCK, HEAD_DIM), lambda b, f: (b, 0)),
            pl.BlockSpec((tokens, HEAD_DIM), lambda b, f: (0, 1)),
            pl.BlockSpec((tokens, HEAD_DIM), lambda b, f: (0, 2)),
            pl.BlockSpec((BLOCK, 1), lambda b, f: (b, 0)),
        ],
        out_specs=pl.BlockSpec((BLOCK, HEAD_DIM), lambda b, f: (b, 0)),
        scratch_shapes=[
            pltpu.VMEM((tiles, BLOCK, BLOCK), jnp.float32),
            pltpu.VMEM((BLOCK, 1), jnp.float32),
            pltpu.VMEM((BLOCK, 1), jnp.float32),
            pltpu.VMEM((BLOCK, HEAD_DIM), jnp.float32),
        ],
    )
    block_firsts = doc_start.reshape(tokens // BLOCK, BLOCK)[:, 0]
    return pl.pallas_call(
        functools.partial(attn_kernel, doc_most),
        grid_spec=grid_spec,
        out_shape=jax.ShapeDtypeStruct((tokens, HEAD_DIM), jnp.bfloat16),
    )(block_firsts, rows, rows, rows, doc_start.reshape(tokens, 1))


def per_device(queries, keys, values, order, doc_lengths):
    nz = lax.axis_size("z")
    ny = lax.axis_size("y")
    tok_rows = queries.shape[0]
    tokens = tok_rows * nz * ny
    query_split = queries.reshape(tok_rows, HEADS, HEAD_DIM)
    query_heads = lax.all_to_all(query_split, ("z", "y"), split_axis=1, concat_axis=0, tiled=True)
    q_slots = query_heads.reshape(nz, ny, tok_rows, HEAD_DIM)
    q_ring = jnp.transpose(q_slots, (1, 0, 2, 3)).reshape(tokens, HEAD_DIM)
    paired = jnp.stack(
        [keys.reshape(tok_rows, KV_HEADS, HEAD_DIM), values.reshape(tok_rows, KV_HEADS, HEAD_DIM)],
        axis=2,
    )
    kv_col = lax.all_to_all(paired, "z", split_axis=1, concat_axis=0, tiled=True)
    kv_ring = lax.all_gather(kv_col, "y", axis=0, tiled=True).reshape(tokens, 2 * HEAD_DIM)
    joined = jnp.concatenate([q_ring, kv_ring], axis=1)
    doc_most = tokens // 8
    slot_ids = jnp.arange(tokens, dtype=jnp.int32)
    _, slot_of = lax.sort((order, slot_ids), num_keys=1)
    slot_dev = slot_of // tok_rows
    ring_row = (slot_dev % ny) * (nz * tok_rows) + (slot_dev // ny) * tok_rows + slot_of % tok_rows
    pos_rows = joined.at[ring_row].get(mode="promise_in_bounds", unique_indices=True)
    doc_start = document_starts(doc_lengths, tokens)
    context = attend(pos_rows, doc_start, doc_most)
    slotted = context.at[order].get(mode="promise_in_bounds", unique_indices=True)
    returned = lax.all_to_all(slotted, ("z", "y"), split_axis=0, concat_axis=1, tiled=True)
    return returned.reshape(tok_rows, HEADS * HEAD_DIM)


def solution(mesh):
    dp_size, ctx_size = mesh.devices.shape
    grid = Mesh(mesh.devices.reshape(dp_size, KV_HEADS, ctx_size // KV_HEADS), ("dp", "z", "y"))
    rows = P(("dp", "z", "y"), None)
    placed = (rows, rows, rows, P("dp"), P("dp"))
    return jax.shard_map(per_device, mesh=grid, in_specs=placed, out_specs=rows, check_vma=False)
```

```python
import functools

import jax
import jax.numpy as jnp
from jax import lax
from jax.experimental import pallas as pl
from jax.experimental.pallas import tpu as pltpu
from jax.sharding import Mesh
from jax.sharding import PartitionSpec as P

HEADS = 64
KV_HEADS = 8
HEAD_DIM = 128
BLOCK = 512


def document_starts(doc_lengths, tokens):
    doc_count = doc_lengths.shape[0]
    doc_ends = jnp.cumsum(doc_lengths)
    positions = jnp.arange(tokens, dtype=jnp.int32)
    doc_index = jnp.sum((positions[:, None] >= doc_ends[None, :]).astype(jnp.int32), axis=1)
    doc_firsts = doc_ends - doc_lengths
    matches = doc_index[:, None] == jnp.arange(doc_count, dtype=jnp.int32)[None, :]
    return jnp.sum(jnp.where(matches, doc_firsts[None, :], 0), axis=1)


def attn_kernel(doc_most, first_ref, *refs):
    tiles = doc_most // BLOCK + 1
    q_ref = refs[0]
    k_refs = refs[1 : 1 + tiles]
    v_refs = refs[1 + tiles : 1 + 2 * tiles]
    ds_ref, o_ref, s_scr, m_scr, l_scr, acc_scr = refs[1 + 2 * tiles :]
    b = pl.program_id(0)
    start = pl.multiple_of(jnp.maximum(b * BLOCK - doc_most, 0), BLOCK)
    q_first = b * BLOCK
    ds_first = first_ref[b]
    q = q_ref[...]
    qpos = q_first + lax.broadcasted_iota(jnp.int32, (BLOCK, BLOCK), 0)
    ds = ds_ref[...]
    m_scr[...] = jnp.full(m_scr.shape, -jnp.inf, jnp.float32)
    l_scr[...] = jnp.zeros(l_scr.shape, jnp.float32)
    acc_scr[...] = jnp.zeros(acc_scr.shape, jnp.float32)
    needed = []
    for t in range(tiles):
        key_first = start + t * BLOCK
        needed.append((key_first + BLOCK - 1 >= ds_first) & (key_first <= q_first + BLOCK - 1))
    for t in range(tiles):
        key_first = start + t * BLOCK

        @pl.when(needed[t])
        def _():
            k = k_refs[t][...]
            s = lax.dot_general(q, k, (((1,), (1,)), ((), ())), preferred_element_type=jnp.float32)
            s = s * (HEAD_DIM ** (-0.5))
            kpos = key_first + lax.broadcasted_iota(jnp.int32, (BLOCK, BLOCK), 1)
            s = jnp.where((kpos <= qpos) & (kpos >= ds), s, -jnp.inf)
            s_scr[t] = s
            m_scr[...] = jnp.maximum(m_scr[...], jnp.max(s, axis=1, keepdims=True))
    for t in range(tiles):
        @pl.when(needed[t])
        def _():
            e = jnp.exp(s_scr[t] - m_scr[...])
            s_scr[t] = e
            l_scr[...] += jnp.sum(e, axis=1, keepdims=True)
    l_scr[...] = 1.0 / l_scr[...]
    for t in range(tiles):
        key_first = start + t * BLOCK

        @pl.when(needed[t])
        def _():
            v = v_refs[t][...]
            w = (s_scr[t] * l_scr[...]).astype(jnp.bfloat16)
            acc_scr[...] += jnp.dot(w, v, preferred_element_type=jnp.float32)
    o_ref[...] = acc_scr[...].astype(o_ref.dtype)


def attend(rows, doc_start, doc_most):
    tokens = rows.shape[0]
    tiles = doc_most // BLOCK + 1
    lead = doc_most // BLOCK

    def key_tile(t, column):
        return pl.BlockSpec((BLOCK, HEAD_DIM), lambda b, f: (jnp.maximum(b - lead, 0) + t, column))

    grid_spec = pltpu.PrefetchScalarGridSpec(
        num_scalar_prefetch=1,
        grid=(tokens // BLOCK,),
        in_specs=[
            pl.BlockSpec((BLOCK, HEAD_DIM), lambda b, f: (b, 0)),
        ]
        + [key_tile(t, 1) for t in range(tiles)]
        + [key_tile(t, 2) for t in range(tiles)]
        + [pl.BlockSpec((BLOCK, 1), lambda b, f: (b, 0))],
        out_specs=pl.BlockSpec((BLOCK, HEAD_DIM), lambda b, f: (b, 0)),
        scratch_shapes=[
            pltpu.VMEM((tiles, BLOCK, BLOCK), jnp.float32),
            pltpu.VMEM((BLOCK, 1), jnp.float32),
            pltpu.VMEM((BLOCK, 1), jnp.float32),
            pltpu.VMEM((BLOCK, HEAD_DIM), jnp.float32),
        ],
    )
    block_firsts = doc_start.reshape(tokens // BLOCK, BLOCK)[:, 0]
    return pl.pallas_call(
        functools.partial(attn_kernel, doc_most),
        grid_spec=grid_spec,
        out_shape=jax.ShapeDtypeStruct((tokens, HEAD_DIM), jnp.bfloat16),
    )(block_firsts, *([rows] * (1 + 2 * tiles)), doc_start.reshape(tokens, 1))


def per_device(queries, keys, values, order, doc_lengths):
    nz = lax.axis_size("z")
    ny = lax.axis_size("y")
    tok_rows = queries.shape[0]
    tokens = tok_rows * nz * ny
    query_split = queries.reshape(tok_rows, HEADS, HEAD_DIM)
    query_heads = lax.all_to_all(query_split, ("z", "y"), split_axis=1, concat_axis=0, tiled=True)
    q_slots = query_heads.reshape(nz, ny, tok_rows, HEAD_DIM)
    q_ring = jnp.transpose(q_slots, (1, 0, 2, 3)).reshape(tokens, HEAD_DIM)
    paired = jnp.stack(
        [keys.reshape(tok_rows, KV_HEADS, HEAD_DIM), values.reshape(tok_rows, KV_HEADS, HEAD_DIM)],
        axis=2,
    )
    kv_col = lax.all_to_all(paired, "z", split_axis=1, concat_axis=0, tiled=True)
    kv_ring = lax.all_gather(kv_col, "y", axis=0, tiled=True).reshape(tokens, 2 * HEAD_DIM)
    joined = jnp.concatenate([q_ring, kv_ring], axis=1)
    doc_most = tokens // 8
    slot_ids = jnp.arange(tokens, dtype=jnp.int32)
    _, slot_of = lax.sort((order, slot_ids), num_keys=1)
    slot_dev = slot_of // tok_rows
    ring_row = (slot_dev % ny) * (nz * tok_rows) + (slot_dev // ny) * tok_rows + slot_of % tok_rows
    pos_rows = joined.at[ring_row].get(mode="promise_in_bounds", unique_indices=True)
    doc_start = document_starts(doc_lengths, tokens)
    context = attend(pos_rows, doc_start, doc_most)
    slotted = context.at[order].get(mode="promise_in_bounds", unique_indices=True)
    returned = lax.all_to_all(slotted, ("z", "y"), split_axis=0, concat_axis=1, tiled=True)
    return returned.reshape(tok_rows, HEADS * HEAD_DIM)


def solution(mesh):
    dp_size, ctx_size = mesh.devices.shape
    grid = Mesh(mesh.devices.reshape(dp_size, KV_HEADS, ctx_size // KV_HEADS), ("dp", "z", "y"))
    rows = P(("dp", "z", "y"), None)
    placed = (rows, rows, rows, P("dp"), P("dp"))
    return jax.shard_map(per_device, mesh=grid, in_specs=placed, out_specs=rows, check_vma=False)
```

```python
import functools

import jax
import jax.numpy as jnp
from jax import lax
from jax.experimental import pallas as pl
from jax.experimental.pallas import tpu as pltpu
from jax.sharding import Mesh
from jax.sharding import PartitionSpec as P

HEADS = 64
KV_HEADS = 8
HEAD_DIM = 128
BLOCK = 512


def document_starts(doc_lengths, tokens):
    doc_count = doc_lengths.shape[0]
    doc_ends = jnp.cumsum(doc_lengths)
    positions = jnp.arange(tokens, dtype=jnp.int32)
    doc_index = jnp.sum((positions[:, None] >= doc_ends[None, :]).astype(jnp.int32), axis=1)
    doc_firsts = doc_ends - doc_lengths
    matches = doc_index[:, None] == jnp.arange(doc_count, dtype=jnp.int32)[None, :]
    return jnp.sum(jnp.where(matches, doc_firsts[None, :], 0), axis=1)


def attn_kernel(doc_most, first_ref, q_ref, k_ref, v_ref, ds_ref, o_ref, m_scr, l_scr, acc_scr):
    b = pl.program_id(0)
    tiles = doc_most // BLOCK + 1
    start = pl.multiple_of(jnp.maximum(b * BLOCK - doc_most, 0), BLOCK)
    q_first = b * BLOCK
    ds_first = first_ref[b]
    q = q_ref[...]
    qpos = q_first + lax.broadcasted_iota(jnp.int32, (BLOCK, BLOCK), 0)
    ds = ds_ref[...]
    m_scr[...] = jnp.full(m_scr.shape, -1e30, jnp.float32)
    l_scr[...] = jnp.zeros(l_scr.shape, jnp.float32)
    acc_scr[...] = jnp.zeros(acc_scr.shape, jnp.float32)
    needed = []
    for t in range(tiles):
        key_first = start + t * BLOCK
        needed.append((key_first + BLOCK - 1 >= ds_first) & (key_first <= q_first + BLOCK - 1))
    for t in range(tiles):
        key_first = start + t * BLOCK

        @pl.when(needed[t])
        def _():
            k = k_ref[pl.ds(pl.multiple_of(key_first, BLOCK), BLOCK), :]
            v = v_ref[pl.ds(pl.multiple_of(key_first, BLOCK), BLOCK), :]
            s = lax.dot_general(q, k, (((1,), (1,)), ((), ())), preferred_element_type=jnp.float32)
            s = s * (HEAD_DIM ** (-0.5))
            kpos = key_first + lax.broadcasted_iota(jnp.int32, (BLOCK, BLOCK), 1)
            s = jnp.where((kpos <= qpos) & (kpos >= ds), s, -jnp.inf)
            m_old = m_scr[...]
            m_new = jnp.maximum(m_old, jnp.max(s, axis=1, keepdims=True))
            rescale = jnp.exp(m_old - m_new)
            e = jnp.exp(s - m_new)
            l_scr[...] = l_scr[...] * rescale + jnp.sum(e, axis=1, keepdims=True)
            acc_scr[...] = acc_scr[...] * rescale + jnp.dot(
                e.astype(jnp.bfloat16), v, preferred_element_type=jnp.float32
            )
            m_scr[...] = m_new
    acc_scr[...] = acc_scr[...] * (1.0 / l_scr[...])
    o_ref[...] = acc_scr[...].astype(o_ref.dtype)


def attend(rows, doc_start, doc_most):
    tokens = rows.shape[0]
    tiles = doc_most // BLOCK + 1
    grid_spec = pltpu.PrefetchScalarGridSpec(
        num_scalar_prefetch=1,
        grid=(tokens // BLOCK,),
        in_specs=[
            pl.BlockSpec((BLOCK, HEAD_DIM), lambda b, f: (b, 0)),
            pl.BlockSpec((tokens, HEAD_DIM), lambda b, f: (0, 1)),
            pl.BlockSpec((tokens, HEAD_DIM), lambda b, f: (0, 2)),
            pl.BlockSpec((BLOCK, 1), lambda b, f: (b, 0)),
        ],
        out_specs=pl.BlockSpec((BLOCK, HEAD_DIM), lambda b, f: (b, 0)),
        scratch_shapes=[
            pltpu.VMEM((BLOCK, 1), jnp.float32),
            pltpu.VMEM((BLOCK, 1), jnp.float32),
            pltpu.VMEM((BLOCK, HEAD_DIM), jnp.float32),
        ],
    )
    block_firsts = doc_start.reshape(tokens // BLOCK, BLOCK)[:, 0]
    return pl.pallas_call(
        functools.partial(attn_kernel, doc_most),
        grid_spec=grid_spec,
        out_shape=jax.ShapeDtypeStruct((tokens, HEAD_DIM), jnp.bfloat16),
    )(block_firsts, rows, rows, rows, doc_start.reshape(tokens, 1))


def per_device(queries, keys, values, order, doc_lengths):
    nz = lax.axis_size("z")
    ny = lax.axis_size("y")
    tok_rows = queries.shape[0]
    tokens = tok_rows * nz * ny
    query_split = queries.reshape(tok_rows, HEADS, HEAD_DIM)
    query_heads = lax.all_to_all(query_split, ("z", "y"), split_axis=1, concat_axis=0, tiled=True)
    q_slots = query_heads.reshape(nz, ny, tok_rows, HEAD_DIM)
    q_ring = jnp.transpose(q_slots, (1, 0, 2, 3)).reshape(tokens, HEAD_DIM)
    paired = jnp.stack(
        [keys.reshape(tok_rows, KV_HEADS, HEAD_DIM), values.reshape(tok_rows, KV_HEADS, HEAD_DIM)],
        axis=2,
    )
    kv_col = lax.all_to_all(paired, "z", split_axis=1, concat_axis=0, tiled=True)
    kv_ring = lax.all_gather(kv_col, "y", axis=0, tiled=True).reshape(tokens, 2 * HEAD_DIM)
    joined = jnp.concatenate([q_ring, kv_ring], axis=1)
    doc_most = tokens // 8
    slot_ids = jnp.arange(tokens, dtype=jnp.int32)
    _, slot_of = lax.sort((order, slot_ids), num_keys=1)
    slot_dev = slot_of // tok_rows
    ring_row = (slot_dev % ny) * (nz * tok_rows) + (slot_dev // ny) * tok_rows + slot_of % tok_rows
    pos_rows = joined.at[ring_row].get(mode="promise_in_bounds", unique_indices=True)
    doc_start = document_starts(doc_lengths, tokens)
    context = attend(pos_rows, doc_start, doc_most)
    slotted = context.at[order].get(mode="promise_in_bounds", unique_indices=True)
    returned = lax.all_to_all(slotted, ("z", "y"), split_axis=0, concat_axis=1, tiled=True)
    return returned.reshape(tok_rows, HEADS * HEAD_DIM)


def solution(mesh):
    dp_size, ctx_size = mesh.devices.shape
    grid = Mesh(mesh.devices.reshape(dp_size, KV_HEADS, ctx_size // KV_HEADS), ("dp", "z", "y"))
    rows = P(("dp", "z", "y"), None)
    placed = (rows, rows, rows, P("dp"), P("dp"))
    return jax.shard_map(per_device, mesh=grid, in_specs=placed, out_specs=rows, check_vma=False)
```

```python
import functools

import jax
import jax.numpy as jnp
from jax import lax
from jax.experimental import pallas as pl
from jax.experimental.pallas import tpu as pltpu
from jax.sharding import Mesh
from jax.sharding import PartitionSpec as P

HEADS = 64
KV_HEADS = 8
HEAD_DIM = 128
BLOCK = 512


def document_starts(doc_lengths, tokens):
    doc_count = doc_lengths.shape[0]
    doc_ends = jnp.cumsum(doc_lengths)
    positions = jnp.arange(tokens, dtype=jnp.int32)
    doc_index = jnp.sum((positions[:, None] >= doc_ends[None, :]).astype(jnp.int32), axis=1)
    doc_firsts = doc_ends - doc_lengths
    matches = doc_index[:, None] == jnp.arange(doc_count, dtype=jnp.int32)[None, :]
    return jnp.sum(jnp.where(matches, doc_firsts[None, :], 0), axis=1)


def attn_kernel(doc_most, first_ref, q_ref, k_ref, v_ref, ds_ref, o_ref, s_scr, m_scr, l_scr, acc_scr):
    b = pl.program_id(0)
    tiles = doc_most // BLOCK + 1
    start = pl.multiple_of(jnp.maximum(b * BLOCK - doc_most, 0), BLOCK)
    q_first = b * BLOCK
    ds_first = first_ref[b]
    q = q_ref[...]
    qpos = q_first + lax.broadcasted_iota(jnp.int32, (BLOCK, BLOCK), 0)
    ds = ds_ref[...]
    m_scr[...] = jnp.full(m_scr.shape, -jnp.inf, jnp.float32)
    l_scr[...] = jnp.zeros(l_scr.shape, jnp.float32)
    acc_scr[...] = jnp.zeros(acc_scr.shape, jnp.float32)
    needed = []
    for t in range(tiles):
        key_first = start + t * BLOCK
        needed.append((key_first + BLOCK - 1 >= ds_first) & (key_first <= q_first + BLOCK - 1))
    for t in range(tiles):
        key_first = start + t * BLOCK

        @pl.when(needed[t])
        def _():
            k = k_ref[pl.ds(pl.multiple_of(key_first, BLOCK), BLOCK), :]
            s = lax.dot_general(q, k, (((1,), (1,)), ((), ())), preferred_element_type=jnp.float32)
            s = s * (HEAD_DIM ** (-0.5))
            kpos = key_first + lax.broadcasted_iota(jnp.int32, (BLOCK, BLOCK), 1)
            s = jnp.where((kpos <= qpos) & (kpos >= ds), s, -jnp.inf)
            s_scr[t] = s
            m_scr[...] = jnp.maximum(m_scr[...], jnp.max(s, axis=1, keepdims=True))
    for t in range(tiles):
        @pl.when(needed[t])
        def _():
            e = jnp.exp(s_scr[t] - m_scr[...])
            s_scr[t] = e
            l_scr[...] += jnp.sum(e, axis=1, keepdims=True)
    l_scr[...] = 1.0 / l_scr[...]
    for t in range(tiles):
        key_first = start + t * BLOCK

        @pl.when(needed[t])
        def _():
            v = v_ref[pl.ds(pl.multiple_of(key_first, BLOCK), BLOCK), :]
            w = (s_scr[t] * l_scr[...]).astype(jnp.bfloat16)
            acc_scr[...] += jnp.dot(w, v, preferred_element_type=jnp.float32)
    o_ref[...] = acc_scr[...].astype(o_ref.dtype)


def attend(rows, doc_start, doc_most):
    tokens = rows.shape[0]
    tiles = doc_most // BLOCK + 1
    grid_spec = pltpu.PrefetchScalarGridSpec(
        num_scalar_prefetch=1,
        grid=(tokens // BLOCK,),
        in_specs=[
            pl.BlockSpec((BLOCK, HEAD_DIM), lambda b, f: (b, 0)),
            pl.BlockSpec((tokens, HEAD_DIM), lambda b, f: (0, 1)),
            pl.BlockSpec((tokens, HEAD_DIM), lambda b, f: (0, 2)),
            pl.BlockSpec((BLOCK, 1), lambda b, f: (b, 0)),
        ],
        out_specs=pl.BlockSpec((BLOCK, HEAD_DIM), lambda b, f: (b, 0)),
        scratch_shapes=[
            pltpu.VMEM((tiles, BLOCK, BLOCK), jnp.float32),
            pltpu.VMEM((BLOCK, 1), jnp.float32),
            pltpu.VMEM((BLOCK, 1), jnp.float32),
            pltpu.VMEM((BLOCK, HEAD_DIM), jnp.float32),
        ],
    )
    block_firsts = doc_start.reshape(tokens // BLOCK, BLOCK)[:, 0]
    return pl.pallas_call(
        functools.partial(attn_kernel, doc_most),
        grid_spec=grid_spec,
        out_shape=jax.ShapeDtypeStruct((tokens, HEAD_DIM), jnp.bfloat16),
    )(block_firsts, rows, rows, rows, doc_start.reshape(tokens, 1))


def per_device(queries, keys, values, order, doc_lengths):
    nz = lax.axis_size("z")
    ny = lax.axis_size("y")
    tok_rows = queries.shape[0]
    tokens = tok_rows * nz * ny
    query_split = queries.reshape(tok_rows, HEADS, HEAD_DIM)
    query_heads = lax.all_to_all(query_split, ("z", "y"), split_axis=1, concat_axis=0, tiled=True)
    q_slots = query_heads.reshape(nz, ny, tok_rows, HEAD_DIM)
    q_ring = jnp.transpose(q_slots, (1, 0, 2, 3)).reshape(tokens, HEAD_DIM)
    paired = jnp.concatenate(
        [keys.reshape(tok_rows, KV_HEADS, HEAD_DIM), values.reshape(tok_rows, KV_HEADS, HEAD_DIM)],
        axis=2,
    )
    kv_col = lax.all_to_all(paired, "z", split_axis=1, concat_axis=0, tiled=True)
    kv_ring = lax.all_gather(kv_col, "y", axis=0, tiled=True).reshape(tokens, 2 * HEAD_DIM)
    joined = jnp.concatenate([q_ring, kv_ring], axis=1)
    doc_most = tokens // 8
    slot_ids = jnp.arange(tokens, dtype=jnp.int32)
    _, slot_of = lax.sort((order, slot_ids), num_keys=1)
    slot_dev = slot_of // tok_rows
    ring_row = (slot_dev % ny) * (nz * tok_rows) + (slot_dev // ny) * tok_rows + slot_of % tok_rows
    pos_rows = joined.at[ring_row].get(mode="promise_in_bounds", unique_indices=True)
    doc_start = document_starts(doc_lengths, tokens)
    context = attend(pos_rows, doc_start, doc_most)
    slotted = context.at[order].get(mode="promise_in_bounds", unique_indices=True)
    returned = lax.all_to_all(slotted, ("z", "y"), split_axis=0, concat_axis=1, tiled=True)
    return returned.reshape(tok_rows, HEADS * HEAD_DIM)


def solution(mesh):
    dp_size, ctx_size = mesh.devices.shape
    grid = Mesh(mesh.devices.reshape(dp_size, KV_HEADS, ctx_size // KV_HEADS), ("dp", "z", "y"))
    rows = P(("dp", "z", "y"), None)
    placed = (rows, rows, rows, P("dp"), P("dp"))
    return jax.shard_map(per_device, mesh=grid, in_specs=placed, out_specs=rows, check_vma=False)
```

```python
import functools

import jax
import jax.numpy as jnp
from jax import lax
from jax.experimental import pallas as pl
from jax.experimental.pallas import tpu as pltpu
from jax.sharding import Mesh
from jax.sharding import PartitionSpec as P

HEADS = 64
KV_HEADS = 8
HEAD_DIM = 128
BLOCK = 512


def document_starts(doc_lengths, tokens):
    doc_count = doc_lengths.shape[0]
    doc_ends = jnp.cumsum(doc_lengths)
    positions = jnp.arange(tokens, dtype=jnp.int32)
    doc_index = jnp.sum((positions[:, None] >= doc_ends[None, :]).astype(jnp.int32), axis=1)
    doc_firsts = doc_ends - doc_lengths
    matches = doc_index[:, None] == jnp.arange(doc_count, dtype=jnp.int32)[None, :]
    return jnp.sum(jnp.where(matches, doc_firsts[None, :], 0), axis=1)


def attn_kernel(doc_most, first_ref, q_ref, k_ref, v_ref, ds_ref, o_ref, s_scr, m_scr, l_scr, acc_scr):
    b = pl.program_id(0)
    tiles = doc_most // BLOCK + 1
    start = pl.multiple_of(jnp.maximum(b * BLOCK - doc_most, 0), BLOCK)
    q_first = b * BLOCK
    ds_first = first_ref[b]
    q = q_ref[...]
    qpos = q_first + lax.broadcasted_iota(jnp.int32, (BLOCK, BLOCK), 0)
    ds = ds_ref[...]
    m_scr[...] = jnp.full(m_scr.shape, -jnp.inf, jnp.float32)
    l_scr[...] = jnp.zeros(l_scr.shape, jnp.float32)
    acc_scr[...] = jnp.zeros(acc_scr.shape, jnp.float32)
    needed = []
    for t in range(tiles):
        key_first = start + t * BLOCK
        needed.append((key_first + BLOCK - 1 >= ds_first) & (key_first <= q_first + BLOCK - 1))
    for t in range(tiles):
        key_first = start + t * BLOCK

        @pl.when(needed[t])
        def _():
            k = k_ref[pl.ds(pl.multiple_of(key_first, BLOCK), BLOCK), :]
            s = lax.dot_general(q, k, (((1,), (1,)), ((), ())), preferred_element_type=jnp.float32)
            s = s * (HEAD_DIM ** (-0.5))
            kpos = key_first + lax.broadcasted_iota(jnp.int32, (BLOCK, BLOCK), 1)
            s = jnp.where((kpos <= qpos) & (kpos >= ds), s, -jnp.inf)
            s_scr[t] = s
            m_scr[...] = jnp.maximum(m_scr[...], jnp.max(s, axis=1, keepdims=True))
    for t in range(tiles):
        @pl.when(needed[t])
        def _():
            e = jnp.exp(s_scr[t] - m_scr[...])
            s_scr[t] = e
            l_scr[...] += jnp.sum(e, axis=1, keepdims=True)
    l_scr[...] = 1.0 / l_scr[...]
    for t in range(tiles):
        key_first = start + t * BLOCK

        @pl.when(needed[t])
        def _():
            v = v_ref[pl.ds(pl.multiple_of(key_first, BLOCK), BLOCK), :]
            w = (s_scr[t] * l_scr[...]).astype(jnp.bfloat16)
            acc_scr[...] += jnp.dot(w, v, preferred_element_type=jnp.float32)
    o_ref[...] = acc_scr[...].astype(o_ref.dtype)


def attend(rows, doc_start, doc_most):
    tokens = rows.shape[0]
    tiles = doc_most // BLOCK + 1
    grid_spec = pltpu.PrefetchScalarGridSpec(
        num_scalar_prefetch=1,
        grid=(tokens // BLOCK,),
        in_specs=[
            pl.BlockSpec((BLOCK, HEAD_DIM), lambda b, f: (b, 0)),
            pl.BlockSpec((tokens, HEAD_DIM), lambda b, f: (0, 1)),
            pl.BlockSpec((tokens, HEAD_DIM), lambda b, f: (0, 2)),
            pl.BlockSpec((BLOCK, 1), lambda b, f: (b, 0)),
        ],
        out_specs=pl.BlockSpec((BLOCK, HEAD_DIM), lambda b, f: (b, 0)),
        scratch_shapes=[
            pltpu.VMEM((tiles, BLOCK, BLOCK), jnp.float32),
            pltpu.VMEM((BLOCK, 1), jnp.float32),
            pltpu.VMEM((BLOCK, 1), jnp.float32),
            pltpu.VMEM((BLOCK, HEAD_DIM), jnp.float32),
        ],
    )
    block_firsts = doc_start.reshape(tokens // BLOCK, BLOCK)[:, 0]
    return pl.pallas_call(
        functools.partial(attn_kernel, doc_most),
        grid_spec=grid_spec,
        out_shape=jax.ShapeDtypeStruct((tokens, HEAD_DIM), jnp.bfloat16),
    )(block_firsts, rows, rows, rows, doc_start.reshape(tokens, 1))


def per_device(queries, keys, values, order, doc_lengths):
    nz = lax.axis_size("z")
    ny = lax.axis_size("y")
    tok_rows = queries.shape[0]
    tokens = tok_rows * nz * ny
    query_split = queries.reshape(tok_rows, HEADS, HEAD_DIM)
    query_heads = lax.all_to_all(query_split, ("z", "y"), split_axis=1, concat_axis=0, tiled=True)
    q_slots = query_heads.reshape(nz, ny, tok_rows, HEAD_DIM)
    q_ring = jnp.transpose(q_slots, (1, 0, 2, 3)).reshape(tokens, HEAD_DIM)
    paired = jnp.concatenate(
        [keys.reshape(tok_rows, KV_HEADS, HEAD_DIM), values.reshape(tok_rows, KV_HEADS, HEAD_DIM)],
        axis=2,
    )
    kv_col = lax.all_to_all(paired, "z", split_axis=1, concat_axis=0, tiled=True)
    kv_ring = lax.all_gather(kv_col, "y", axis=0, tiled=True).reshape(tokens, 2 * HEAD_DIM)
    joined = jnp.zeros((tokens, 3 * HEAD_DIM), q_ring.dtype).at[:, :HEAD_DIM].set(q_ring)
    joined = lax.optimization_barrier(joined)
    joined = lax.dynamic_update_slice(joined, kv_ring, (0, HEAD_DIM))
    doc_most = tokens // 8
    slot_ids = jnp.arange(tokens, dtype=jnp.int32)
    _, slot_of = lax.sort((order, slot_ids), num_keys=1)
    slot_dev = slot_of // tok_rows
    ring_row = (slot_dev % ny) * (nz * tok_rows) + (slot_dev // ny) * tok_rows + slot_of % tok_rows
    pos_rows = joined.at[ring_row].get(mode="promise_in_bounds", unique_indices=True)
    doc_start = document_starts(doc_lengths, tokens)
    context = attend(pos_rows, doc_start, doc_most)
    slotted = context.at[order].get(mode="promise_in_bounds", unique_indices=True)
    returned = lax.all_to_all(slotted, ("z", "y"), split_axis=0, concat_axis=1, tiled=True)
    return returned.reshape(tok_rows, HEADS * HEAD_DIM)


def solution(mesh):
    dp_size, ctx_size = mesh.devices.shape
    grid = Mesh(mesh.devices.reshape(dp_size, KV_HEADS, ctx_size // KV_HEADS), ("dp", "z", "y"))
    rows = P(("dp", "z", "y"), None)
    placed = (rows, rows, rows, P("dp"), P("dp"))
    return jax.shard_map(per_device, mesh=grid, in_specs=placed, out_specs=rows, check_vma=False)
```

```python
import functools

import jax
import jax.numpy as jnp
from jax import lax
from jax.experimental import pallas as pl
from jax.experimental.pallas import tpu as pltpu
from jax.sharding import Mesh
from jax.sharding import PartitionSpec as P

HEADS = 64
KV_HEADS = 8
HEAD_DIM = 128
BLOCK = 512


def document_starts(doc_lengths, tokens):
    doc_count = doc_lengths.shape[0]
    doc_ends = jnp.cumsum(doc_lengths)
    positions = jnp.arange(tokens, dtype=jnp.int32)
    doc_index = jnp.sum((positions[:, None] >= doc_ends[None, :]).astype(jnp.int32), axis=1)
    doc_firsts = doc_ends - doc_lengths
    matches = doc_index[:, None] == jnp.arange(doc_count, dtype=jnp.int32)[None, :]
    return jnp.sum(jnp.where(matches, doc_firsts[None, :], 0), axis=1)


def attn_kernel(doc_most, first_ref, q_ref, k_ref, v_ref, ds_ref, o_ref, s_scr, m_scr, l_scr, acc_scr):
    b = pl.program_id(0)
    tiles = doc_most // BLOCK + 1
    start = pl.multiple_of(jnp.maximum(b * BLOCK - doc_most, 0), BLOCK)
    q_first = b * BLOCK
    ds_first = first_ref[b]
    q = q_ref[...]
    row_pos = q_first + lax.broadcasted_iota(jnp.int32, (BLOCK, 1), 0)
    col = lax.broadcasted_iota(jnp.int32, (BLOCK, BLOCK), 1)
    ds = ds_ref[...]
    m_scr[...] = jnp.full(m_scr.shape, -jnp.inf, jnp.float32)
    l_scr[...] = jnp.zeros(l_scr.shape, jnp.float32)
    acc_scr[...] = jnp.zeros(acc_scr.shape, jnp.float32)
    needed = []
    for t in range(tiles):
        key_first = start + t * BLOCK
        needed.append((key_first + BLOCK - 1 >= ds_first) & (key_first <= q_first + BLOCK - 1))
    for t in range(tiles):
        key_first = start + t * BLOCK

        @pl.when(needed[t])
        def _():
            k = k_ref[pl.ds(pl.multiple_of(key_first, BLOCK), BLOCK), :]
            s = lax.dot_general(q, k, (((1,), (1,)), ((), ())), preferred_element_type=jnp.float32)
            s = s * (HEAD_DIM ** (-0.5))
            s = jnp.where((col <= row_pos - key_first) & (col >= ds - key_first), s, -jnp.inf)
            s_scr[t] = s
            m_scr[...] = jnp.maximum(m_scr[...], jnp.max(s, axis=1, keepdims=True))
    for t in range(tiles):
        @pl.when(needed[t])
        def _():
            e = jnp.exp(s_scr[t] - m_scr[...])
            s_scr[t] = e
            l_scr[...] += jnp.sum(e, axis=1, keepdims=True)
    l_scr[...] = 1.0 / l_scr[...]
    for t in range(tiles):
        key_first = start + t * BLOCK

        @pl.when(needed[t])
        def _():
            v = v_ref[pl.ds(pl.multiple_of(key_first, BLOCK), BLOCK), :]
            w = (s_scr[t] * l_scr[...]).astype(jnp.bfloat16)
            acc_scr[...] += jnp.dot(w, v, preferred_element_type=jnp.float32)
    o_ref[...] = acc_scr[...].astype(o_ref.dtype)


def attend(rows, doc_start, doc_most):
    tokens = rows.shape[0]
    tiles = doc_most // BLOCK + 1
    grid_spec = pltpu.PrefetchScalarGridSpec(
        num_scalar_prefetch=1,
        grid=(tokens // BLOCK,),
        in_specs=[
            pl.BlockSpec((BLOCK, HEAD_DIM), lambda b, f: (b, 0)),
            pl.BlockSpec((tokens, HEAD_DIM), lambda b, f: (0, 1)),
            pl.BlockSpec((tokens, HEAD_DIM), lambda b, f: (0, 2)),
            pl.BlockSpec((BLOCK, 1), lambda b, f: (b, 0)),
        ],
        out_specs=pl.BlockSpec((BLOCK, HEAD_DIM), lambda b, f: (b, 0)),
        scratch_shapes=[
            pltpu.VMEM((tiles, BLOCK, BLOCK), jnp.float32),
            pltpu.VMEM((BLOCK, 1), jnp.float32),
            pltpu.VMEM((BLOCK, 1), jnp.float32),
            pltpu.VMEM((BLOCK, HEAD_DIM), jnp.float32),
        ],
    )
    block_firsts = doc_start.reshape(tokens // BLOCK, BLOCK)[:, 0]
    return pl.pallas_call(
        functools.partial(attn_kernel, doc_most),
        grid_spec=grid_spec,
        out_shape=jax.ShapeDtypeStruct((tokens, HEAD_DIM), jnp.bfloat16),
    )(block_firsts, rows, rows, rows, doc_start.reshape(tokens, 1))


def per_device(queries, keys, values, order, doc_lengths):
    nz = lax.axis_size("z")
    ny = lax.axis_size("y")
    tok_rows = queries.shape[0]
    tokens = tok_rows * nz * ny
    query_split = queries.reshape(tok_rows, HEADS, HEAD_DIM)
    query_heads = lax.all_to_all(query_split, ("z", "y"), split_axis=1, concat_axis=0, tiled=True)
    q_slots = query_heads.reshape(nz, ny, tok_rows, HEAD_DIM)
    q_ring = jnp.transpose(q_slots, (1, 0, 2, 3)).reshape(tokens, HEAD_DIM)
    paired = jnp.concatenate(
        [keys.reshape(tok_rows, KV_HEADS, HEAD_DIM), values.reshape(tok_rows, KV_HEADS, HEAD_DIM)],
        axis=2,
    )
    kv_col = lax.all_to_all(paired, "z", split_axis=1, concat_axis=0, tiled=True)
    kv_ring = lax.all_gather(kv_col, "y", axis=0, tiled=True).reshape(tokens, 2 * HEAD_DIM)
    joined = jnp.zeros((tokens, 3 * HEAD_DIM), q_ring.dtype).at[:, :HEAD_DIM].set(q_ring)
    joined = lax.optimization_barrier(joined)
    joined = lax.dynamic_update_slice(joined, kv_ring, (0, HEAD_DIM))
    doc_most = tokens // 8
    slot_ids = jnp.arange(tokens, dtype=jnp.int32)
    _, slot_of = lax.sort((order, slot_ids), num_keys=1)
    slot_dev = slot_of // tok_rows
    ring_row = (slot_dev % ny) * (nz * tok_rows) + (slot_dev // ny) * tok_rows + slot_of % tok_rows
    pos_rows = joined.at[ring_row].get(mode="promise_in_bounds", unique_indices=True)
    doc_start = document_starts(doc_lengths, tokens)
    context = attend(pos_rows, doc_start, doc_most)
    slotted = context.at[order].get(mode="promise_in_bounds", unique_indices=True)
    returned = lax.all_to_all(slotted, ("z", "y"), split_axis=0, concat_axis=1, tiled=True)
    return returned.reshape(tok_rows, HEADS * HEAD_DIM)


def solution(mesh):
    dp_size, ctx_size = mesh.devices.shape
    grid = Mesh(mesh.devices.reshape(dp_size, KV_HEADS, ctx_size // KV_HEADS), ("dp", "z", "y"))
    rows = P(("dp", "z", "y"), None)
    placed = (rows, rows, rows, P("dp"), P("dp"))
    return jax.shard_map(per_device, mesh=grid, in_specs=placed, out_specs=rows, check_vma=False)
```

```python
import functools

import jax
import jax.numpy as jnp
from jax import lax
from jax.experimental import pallas as pl
from jax.experimental.pallas import tpu as pltpu
from jax.sharding import Mesh
from jax.sharding import PartitionSpec as P

HEADS = 64
KV_HEADS = 8
HEAD_DIM = 128
BLOCK = 512


def document_starts(doc_lengths, tokens):
    doc_count = doc_lengths.shape[0]
    doc_ends = jnp.cumsum(doc_lengths)
    positions = jnp.arange(tokens, dtype=jnp.int32)
    doc_index = jnp.sum((positions[:, None] >= doc_ends[None, :]).astype(jnp.int32), axis=1)
    doc_firsts = doc_ends - doc_lengths
    matches = doc_index[:, None] == jnp.arange(doc_count, dtype=jnp.int32)[None, :]
    return jnp.sum(jnp.where(matches, doc_firsts[None, :], 0), axis=1)


def attn_kernel(doc_most, first_ref, q_ref, k_ref, v_ref, ds_ref, o_ref, s_scr, m_scr, l_scr, acc_scr):
    b = pl.program_id(0)
    tiles = doc_most // BLOCK + 1
    start = pl.multiple_of(jnp.maximum(b * BLOCK - doc_most, 0), BLOCK)
    q_first = b * BLOCK
    ds_first = first_ref[b]
    q = q_ref[...]
    qpos = q_first + lax.broadcasted_iota(jnp.int32, (BLOCK, BLOCK), 0)
    ds = ds_ref[...]
    m_scr[...] = jnp.full(m_scr.shape, -jnp.inf, jnp.float32)
    l_scr[...] = jnp.zeros(l_scr.shape, jnp.float32)
    acc_scr[...] = jnp.zeros(acc_scr.shape, jnp.float32)
    needed = []
    for t in range(tiles):
        key_first = start + t * BLOCK
        needed.append((key_first + BLOCK - 1 >= ds_first) & (key_first <= q_first + BLOCK - 1))
    for t in range(tiles):
        key_first = start + t * BLOCK

        @pl.when(needed[t])
        def _():
            k = k_ref[pl.ds(pl.multiple_of(key_first, BLOCK), BLOCK), :]
            s = lax.dot_general(q, k, (((1,), (1,)), ((), ())), preferred_element_type=jnp.float32)
            s = s * (HEAD_DIM ** (-0.5))
            kpos = key_first + lax.broadcasted_iota(jnp.int32, (BLOCK, BLOCK), 1)
            s = jnp.where((kpos <= qpos) & (kpos >= ds), s, -jnp.inf)
            s_scr[t] = s
            m_scr[...] = jnp.maximum(m_scr[...], jnp.max(s, axis=1, keepdims=True))
    for t in range(tiles):
        @pl.when(needed[t])
        def _():
            e = jnp.exp(s_scr[t] - m_scr[...])
            s_scr[t] = e
            l_scr[...] += jnp.sum(e, axis=1, keepdims=True)
    l_scr[...] = 1.0 / l_scr[...]
    for t in range(tiles):
        key_first = start + t * BLOCK

        @pl.when(needed[t])
        def _():
            v = v_ref[pl.ds(pl.multiple_of(key_first, BLOCK), BLOCK), :]
            w = (s_scr[t] * l_scr[...]).astype(jnp.bfloat16)
            acc_scr[...] += jnp.dot(w, v, preferred_element_type=jnp.float32)
    o_ref[...] = acc_scr[...].astype(o_ref.dtype)


def attend(rows, doc_start, doc_most):
    tokens = rows.shape[0]
    tiles = doc_most // BLOCK + 1
    grid_spec = pltpu.PrefetchScalarGridSpec(
        num_scalar_prefetch=1,
        grid=(tokens // BLOCK,),
        in_specs=[
            pl.BlockSpec((BLOCK, HEAD_DIM), lambda b, f: (b, 0)),
            pl.BlockSpec((tokens, HEAD_DIM), lambda b, f: (0, 1)),
            pl.BlockSpec((tokens, HEAD_DIM), lambda b, f: (0, 2)),
            pl.BlockSpec((BLOCK, 1), lambda b, f: (b, 0)),
        ],
        out_specs=pl.BlockSpec((BLOCK, HEAD_DIM), lambda b, f: (b, 0)),
        scratch_shapes=[
            pltpu.VMEM((tiles, BLOCK, BLOCK), jnp.float32),
            pltpu.VMEM((BLOCK, 1), jnp.float32),
            pltpu.VMEM((BLOCK, 1), jnp.float32),
            pltpu.VMEM((BLOCK, HEAD_DIM), jnp.float32),
        ],
    )
    block_firsts = doc_start.reshape(tokens // BLOCK, BLOCK)[:, 0]
    return pl.pallas_call(
        functools.partial(attn_kernel, doc_most),
        grid_spec=grid_spec,
        out_shape=jax.ShapeDtypeStruct((tokens, HEAD_DIM), jnp.bfloat16),
    )(block_firsts, rows, rows, rows, doc_start.reshape(tokens, 1))


def per_device(queries, keys, values, order, doc_lengths):
    nz = lax.axis_size("z")
    ny = lax.axis_size("y")
    tok_rows = queries.shape[0]
    tokens = tok_rows * nz * ny
    query_split = queries.reshape(tok_rows, HEADS, HEAD_DIM)
    query_heads = lax.all_to_all(query_split, ("z", "y"), split_axis=1, concat_axis=0, tiled=True)
    q_slots = query_heads.reshape(nz, ny, tok_rows, HEAD_DIM)
    q_ring = jnp.transpose(q_slots, (1, 0, 2, 3)).reshape(tokens, HEAD_DIM)
    rings = []
    for part in (keys, values):
        split = part.reshape(tok_rows, KV_HEADS, HEAD_DIM)
        col = lax.all_to_all(split, "z", split_axis=1, concat_axis=0, tiled=True)
        rings.append(lax.all_gather(col, "y", axis=0, tiled=True).reshape(tokens, HEAD_DIM))
    joined = jnp.zeros((tokens, 3 * HEAD_DIM), q_ring.dtype).at[:, :HEAD_DIM].set(q_ring)
    joined = lax.optimization_barrier(joined)
    joined = lax.dynamic_update_slice(joined, rings[0], (0, HEAD_DIM))
    joined = lax.dynamic_update_slice(joined, rings[1], (0, 2 * HEAD_DIM))
    doc_most = tokens // 8
    slot_ids = jnp.arange(tokens, dtype=jnp.int32)
    _, slot_of = lax.sort((order, slot_ids), num_keys=1)
    slot_dev = slot_of // tok_rows
    ring_row = (slot_dev % ny) * (nz * tok_rows) + (slot_dev // ny) * tok_rows + slot_of % tok_rows
    pos_rows = joined.at[ring_row].get(mode="promise_in_bounds", unique_indices=True)
    doc_start = document_starts(doc_lengths, tokens)
    context = attend(pos_rows, doc_start, doc_most)
    slotted = context.at[order].get(mode="promise_in_bounds", unique_indices=True)
    returned = lax.all_to_all(slotted, ("z", "y"), split_axis=0, concat_axis=1, tiled=True)
    return returned.reshape(tok_rows, HEADS * HEAD_DIM)


def solution(mesh):
    dp_size, ctx_size = mesh.devices.shape
    grid = Mesh(mesh.devices.reshape(dp_size, KV_HEADS, ctx_size // KV_HEADS), ("dp", "z", "y"))
    rows = P(("dp", "z", "y"), None)
    placed = (rows, rows, rows, P("dp"), P("dp"))
    return jax.shard_map(per_device, mesh=grid, in_specs=placed, out_specs=rows, check_vma=False)
```
